32 devices in a mesh: rad: 32 (over z, y, x, core), lat: 1.
Axes of the slice: x: 2, y: 2, z: 4, core: 2. Of those that a mesh axis runs over, the one named last changes fastest.
Arguments:
- nonlinear_samples: bfloat16 [32, 2, 1536, 3072], P('rad', None, 'lat'), may hold values from -6 to 6
- legendre: bfloat16 [256, 1536, 1024], P('rad', 'lat'), may hold values from -0.15625 to 0.15625
- assign: int32 [256], replicated, may hold values from 0 to 255, each once
- counts: int32 [256], replicated, may hold values from 513 to 1024, as said below
- spectral_state: float32 [1024, 256, 128], P('lat', 'rad'), may hold values from -6 to 6
- inverses: float32 [1024, 4, 8, 8], P('lat'), may hold values from -1 to 1
Outputs:
- advanced: float32 [1024, 256, 128], P('lat', 'rad')
The draws below stay inside these ranges and needn't reach their ends.
Inputs may be any that keep to these rules, and one draw needn't show every extreme that they name: Slot s carries order assign[s]; each order 0 to 255 stands in exactly one slot. counts[m] is at most 1024 - m, and order 0 has 1024 live degrees.
All inputs are finite; a program needn't handle non-finite values.
Results may differ from the reference program's by a relative error of at most 0.0034.
Values may be sent and summed in bfloat16 or wider, within the bound.
No kernel may reach another device: no remote copies, remote signals or barrier semaphores. Data moves between devices by JAX's collectives and lax.ppermute only.
A program may use at most 192 MiB of HBM per device.

```python
import math
import jax
import jax.numpy as jnp
from jax import lax

NPHI = 3072
NLAT = 1536
LMAX = 1024
KB = 8
NR = 32
ORD = 256
NB = 4
LAT_DEV = 1536


def draw_counts(key, part):
    orders = jnp.arange(ORD, dtype=jnp.int32)
    dropped = jax.random.randint(jax.random.fold_in(key, 11), (ORD,), 0, LMAX // 4 + 1, dtype=jnp.int32)
    values = LMAX - orders - dropped
    return jnp.where(orders == 0, LMAX, values).astype(jnp.int32)


def draw_inverses(key, part):
    radial_spacing = 0.65 / (NR + 1)
    block_ids = jnp.arange(NB, dtype=jnp.float32)
    middle = 0.35 + 0.65 * ((block_ids + 0.5) * KB + 0.5) / (NR + 1)
    degree = jnp.arange(LMAX, dtype=jnp.float32)
    scales = 1.0 / (2.0 + 0.5 * radial_spacing * radial_spacing * degree[:, None] * (degree[:, None] + 1.0) / (middle[None, :] * middle[None, :]))
    random_noise_key = jax.random.fold_in(key, 21)
    diag_key = jax.random.fold_in(key, 22)
    noise = 0.45 * jnp.clip(jax.random.normal(random_noise_key, (LMAX, NB, KB, KB), jnp.float32), -3.0, 3.0)
    noise = noise / math.sqrt(KB)
    diagonal = 1.0 + 0.5 * jax.random.uniform(diag_key, (LMAX, NB, 1, KB), jnp.float32)
    identity = jnp.eye(KB, dtype=jnp.float32)
    return (scales[:, :, None, None] * (identity * diagonal + noise)).astype(jnp.float32)


def block_levels(own_key, shape, shards, low, largest):
    loudness, own = 1.0, jax.random.fold_in(own_key, 6)
    for dim, blocks in shards:
        heights = jnp.exp(jax.random.uniform(jax.random.fold_in(own, dim), (blocks,), jnp.float32, low / len(shards), largest / len(shards)))
        loudness = loudness * jnp.repeat(heights, shape[dim] // blocks).reshape([-1 if axis == dim else 1 for axis in range(len(shape))])
    return loudness


def scatter_about(stream_key, dims, scale, most, shards=(), kind=jnp.bfloat16):
    gain = block_levels(stream_key, dims, shards, -0.22, 0.18) if shards else 1.0
    array = jax.random.normal(stream_key, dims, jnp.float32) * scale * gain
    return jnp.minimum(jnp.maximum(array, -most), most).astype(kind)


def setup_inputs(seed: int = 0) -> dict:
    streams_of = jax.random.split(jax.random.key(seed), 7)
    nonlinear_samples = scatter_about(streams_of[0], (NR, 2, NLAT, NPHI), 1.0, 6.0, ((0, 32),))
    legendre = scatter_about(streams_of[1], (ORD, NLAT, LMAX), NLAT ** -0.5, 0.15625, ((0, 32),))
    assign = jax.random.permutation(streams_of[2], ORD).astype(jnp.int32)
    counts = draw_counts(jax.random.fold_in(streams_of[6], 71), 0)
    spectral_state = scatter_about(streams_of[4], (LMAX, ORD, 4 * NR), 1.0, 6.0, ((1, 32),), jnp.float32)
    inverses = draw_inverses(jax.random.fold_in(streams_of[6], 71), 0)
    return dict(nonlinear_samples=nonlinear_samples, legendre=legendre, assign=assign, counts=counts, spectral_state=spectral_state, inverses=inverses)


def trig_table(assign, lon_count):
    longitude = jnp.arange(lon_count, dtype=jnp.int32)
    phases = longitude[:, None] * assign[None, :] % lon_count
    angles = phases.astype(jnp.float32) * (2.0 * math.pi / lon_count)
    normalizing_multiplier = 1.0 / math.sqrt(lon_count)
    cosine = (jnp.cos(angles) * normalizing_multiplier).astype(jnp.bfloat16)
    sine = (-jnp.sin(angles) * normalizing_multiplier).astype(jnp.bfloat16)
    return jnp.stack([cosine, sine], axis=2).reshape(lon_count, 2 * assign.shape[0])

def radial_step(spectral_state, source, inverses, degree):
    deg_rows, slot_count, width = spectral_state.shape
    shell_number = width // 4
    blk_size = inverses.shape[2]
    blk_count = shell_number // blk_size
    field_now = spectral_state.reshape(deg_rows, slot_count, 4, shell_number)
    zero_rim = jnp.zeros((deg_rows, slot_count, 4, 1), jnp.float32)
    outward = jnp.concatenate([field_now[..., 1:], zero_rim], axis=3)
    inward = jnp.concatenate([zero_rim, field_now[..., :-1]], axis=3)
    radial_spacing = 0.65 / (shell_number + 1)
    radius = 0.35 + 0.65 * (jnp.arange(shell_number, dtype=jnp.float32) + 1.0) / (shell_number + 1)
    ratios = radial_spacing / radius
    degree_term = degree[:, None, None, None] * (degree[:, None, None, None] + 1.0)
    central = 0.5 * radial_spacing * radial_spacing * degree_term / (radius * radius)
    right_side = field_now + 0.5 * (outward - 2.0 * field_now + inward) + 0.5 * ratios * (outward - inward)
    right_side = right_side - central * field_now + source.reshape(deg_rows, slot_count, 4, shell_number)
    lower_link = -0.5 * (1.0 - ratios[0::blk_size])
    upper_link = -0.5 * (1.0 + ratios[blk_size - 1::blk_size])
    blocks = jnp.moveaxis(right_side.reshape(deg_rows, slot_count, 4, blk_count, blk_size), 3, 0)
    block_inverse = jnp.moveaxis(inverses, 1, 0)
    first_unit = (jnp.arange(blk_size, dtype=jnp.int32) == 0).astype(jnp.float32)
    start_carry = jnp.zeros((deg_rows, slot_count, 4), jnp.float32)

    def forward(carried, items):
        matrix, block, link = items
        block = block - link * carried[..., None] * first_unit
        result = jnp.einsum('lij,locj->loci', matrix, block, precision=lax.Precision.HIGHEST)
        return (result[..., blk_size - 1], result)

    def inverse_sweep(carried, items):
        matrix, partial_solution, link = items
        result = partial_solution - link * carried[..., None] * matrix[:, None, None, :, blk_size - 1]
        return (result[..., 0], result)
    _, forward_blocks = lax.scan(forward, start_carry, (block_inverse, blocks, lower_link))
    _, solved = lax.scan(inverse_sweep, start_carry, (block_inverse, forward_blocks, upper_link), reverse=True)
    return jnp.moveaxis(solved, 0, 3).reshape(deg_rows, slot_count, 4 * shell_number)

def reference(nonlinear_samples, legendre, assign, counts, spectral_state, inverses):
    table = trig_table(assign, NPHI)

    def transform(sheet):
        flat_rows = sheet.reshape(2 * NLAT, NPHI)
        result = jnp.dot(flat_rows, table, preferred_element_type=jnp.float32)
        return result.astype(jnp.bfloat16).reshape(2, NLAT, ORD, 2)
    fourier_modes = lax.map(transform, nonlinear_samples)
    by_slot = jnp.moveaxis(fourier_modes, 3, 0)
    band_total = NLAT // LAT_DEV

    def analyse(items):
        table_slot, values = items
        legendre_table_bands = table_slot.reshape(band_total, LAT_DEV, LMAX).astype(jnp.float32)
        value_bands = values.reshape(NR, 2, band_total, LAT_DEV, 2).astype(jnp.float32)
        partial_value = jnp.einsum('btl,rfbtk->blfkr', legendre_table_bands, value_bands)
        partial_value = lax.optimization_barrier(partial_value.astype(jnp.bfloat16)).astype(jnp.float32)
        return lax.optimization_barrier(jnp.sum(partial_value, axis=0)).reshape(LMAX, 4 * NR)
    summed = lax.map(analyse, (legendre, by_slot))
    summed = jnp.moveaxis(summed, 0, 1)
    degree_ids = jnp.arange(LMAX, dtype=jnp.int32)
    limits = assign + counts[assign]
    live = (degree_ids[:, None] >= assign[None, :]) & (degree_ids[:, None] < limits[None, :])
    source = jnp.where(live[:, :, None], summed, jnp.zeros_like(summed))
    return radial_step(spectral_state, source, inverses, degree_ids.astype(jnp.float32))
```

```python
import functools
import math

import jax
import jax.numpy as jnp
import numpy as np
from jax import lax
from jax.experimental import pallas as pl
from jax.experimental.pallas import tpu as pltpu
from jax.sharding import PartitionSpec as P

LANES = 128


def trig_factors(orders, quarter, lon_count):
    step = 2.0 * math.pi / lon_count
    coarse_count = lon_count // LANES
    coarse = (orders[:, None] * jnp.arange(coarse_count, dtype=jnp.int32)) % coarse_count * LANES
    fine = orders[:, None] * jnp.arange(LANES, dtype=jnp.int32) + quarter[:, None] * (lon_count // 4)
    coarse_angle = coarse.astype(jnp.float32) * step
    fine_angle = (fine % lon_count).astype(jnp.float32) * step
    scale = 1.0 / math.sqrt(lon_count)
    return (
        jnp.cos(coarse_angle),
        jnp.sin(coarse_angle),
        jnp.cos(fine_angle) * scale,
        jnp.sin(fine_angle) * scale,
    )


def fourier_kernel(ca, sa, cb, sb, x, out, table):
    @pl.when(pl.program_id(0) == 0)
    def _():
        for a in range(ca.shape[1]):
            value = ca[:, a : a + 1] * cb[...] - sa[:, a : a + 1] * sb[...]
            table[:, a * LANES : (a + 1) * LANES] = value.astype(jnp.bfloat16)

    out[...] = lax.dot_general(
        table[...], x[...], (((1,), (1,)), ((), ())), preferred_element_type=jnp.float32
    ).astype(jnp.bfloat16)


def fourier(factors, rows):
    modes = factors[0].shape[0]
    count, lon_count = rows.shape
    tile = 512 if count % 512 == 0 else count
    whole = lambda v: pl.BlockSpec(v.shape, lambda i: (0, 0))
    return pl.pallas_call(
        fourier_kernel,
        grid=(count // tile,),
        in_specs=[whole(v) for v in factors] + [pl.BlockSpec((tile, lon_count), lambda i: (i, 0))],
        out_specs=pl.BlockSpec((modes, tile), lambda i: (0, i)),
        out_shape=jax.ShapeDtypeStruct((modes, count), jnp.bfloat16),
        scratch_shapes=[pltpu.VMEM((modes, lon_count), jnp.bfloat16)],
        name="fourier",
    )(*factors, rows)


def coefficient_rows(inverses, shells):
    degrees, blocks, size, _ = inverses.shape
    spacing = 0.65 / (shells + 1)
    radius = 0.35 + 0.65 * (np.arange(shells) + 1.0) / (shells + 1)
    ratios = spacing / radius
    lower = -0.5 * (1.0 - ratios[0::size])
    upper = -0.5 * (1.0 + ratios[size - 1 :: size])
    inv = jnp.transpose(inverses, (1, 2, 3, 0))
    kinds = []
    for d in range(size):
        kinds.append(jnp.stack([inv[:, i, (i + d) % size] for i in range(size)], axis=1))
    low = jnp.asarray(-lower, jnp.float32)[:, None, None]
    up = jnp.asarray(-upper, jnp.float32)[:, None, None]
    zero = jnp.zeros((1, size, degrees), jnp.float32)
    first = low * inv[:, :, 0]
    last = up * inv[:, :, size - 1]
    wide = lambda v: jnp.broadcast_to(v[:, None], (v.shape[0], size, degrees))
    kinds.append(jnp.concatenate([zero, first[1:]]))
    kinds.append(jnp.concatenate([zero, zero, wide(first[1:-1, size - 1])]))
    kinds.append(jnp.concatenate([last[:-1], zero]))
    kinds.append(jnp.concatenate([wide(last[1:-1, 0]), zero, zero]))
    return jnp.stack(kinds).reshape(len(kinds), blocks * size, degrees)


def spread_kernel(rows, out):
    value = rows[0]
    out[0] = jnp.transpose(jnp.concatenate([value] * (LANES // value.shape[0]), axis=0))


def spread(rows):
    kinds, width, degrees = rows.shape
    return pl.pallas_call(
        spread_kernel,
        grid=(kinds,),
        in_specs=[pl.BlockSpec((1, width, degrees), lambda i: (i, 0, 0))],
        out_specs=pl.BlockSpec((1, degrees, LANES), lambda i: (i, 0, 0)),
        out_shape=jax.ShapeDtypeStruct((kinds, degrees, LANES), jnp.float32),
        name="spread",
    )(rows)


def lane_constants(shells):
    spacing = 0.65 / (shells + 1)
    shell = np.arange(LANES) % shells
    radius = 0.35 + 0.65 * (shell + 1.0) / (shells + 1)
    half = 0.5 * spacing / radius
    table = np.zeros((8, LANES), np.float32)
    table[0] = np.where(shell < shells - 1, 0.5 + half, 0.0)
    table[1] = np.where(shell > 0, 0.5 - half, 0.0)
    table[2] = -0.5 * spacing * spacing / (radius * radius)
    return jnp.asarray(table)


def solve_kernel(bounds, modes, pick, legendre, coef, lanes, state, out, arranged, band, *, first, slots, size):
    slot = pl.program_id(0)
    degrees = legendre.shape[2]
    lat = legendre.shape[1]
    half = arranged.shape[1] // 2

    @pl.when(slot == 0)
    def _():
        for f in range(2):
            part = jnp.dot(
                pick[...], modes[:, f * lat : (f + 1) * lat], preferred_element_type=jnp.float32
            ).astype(jnp.bfloat16)
            for s in range(slots):
                arranged[s, f * half : (f + 1) * half, :] = part[s * half : (s + 1) * half]

    product = jnp.dot(arranged[slot], legendre[0], preferred_element_type=jnp.float32)
    band[...] = jnp.transpose(product.astype(jnp.bfloat16)).astype(jnp.float32)

    mine = first + slot
    low = bounds[0, mine]
    high = bounds[1, mine]
    offset = bounds[2, 0]
    tile = min(64, degrees)
    shape = (tile, LANES)
    lane = lax.broadcasted_iota(jnp.int32, shape, 1)
    group = lane - lane % size
    around = [group + (lane + d) % size for d in range(size)]
    before = jnp.maximum(group - 1, 0)
    after = jnp.minimum(group + size, LANES - 1)
    row = lax.broadcasted_iota(jnp.int32, shape, 0)
    take = lambda v, index: jnp.take_along_axis(v, index, axis=1, mode="promise_in_bounds")

    def piece(n, carry):
        start = pl.multiple_of(n * tile, tile)
        here = pl.ds(start, tile)
        spread_rows = pl.ds(start * 8 + mine, tile, stride=8)
        now = state[spread_rows, :]
        degree = row + (start + offset)
        live = (degree >= low) & (degree < high)
        source = jnp.where(live, band[here, :], 0.0)
        term = (degree * (degree + 1)).astype(jnp.float32)
        right = lanes[0:1, :] * pltpu.roll(now, LANES - 1, 1) + lanes[1:2, :] * pltpu.roll(now, 1, 1)
        right = right + (lanes[2:3, :] * term) * now + source
        value = coef[0, here, :] * right
        for d in range(1, size):
            value = value + coef[d, here, :] * take(right, around[d])
        link = take(value, before)
        chain = link
        for _ in range(2):
            chain = link + coef[size + 1, here, :] * pltpu.roll(chain, size, 1)
        value = value + coef[size, here, :] * chain
        link = take(value, after)
        chain = link
        for _ in range(2):
            chain = link + coef[size + 3, here, :] * pltpu.roll(chain, LANES - size, 1)
        out[spread_rows, :] = value + coef[size + 2, here, :] * chain
        return carry

    lax.fori_loop(0, degrees // tile, piece, 0)


def legendre_solve(bounds, modes, legendre, coef, lanes, state, first, slots, size):
    shells = modes.shape[0] // (2 * slots)
    order, lat, degrees = legendre.shape
    wanted = np.arange(2 * slots * shells)
    place = (wanted % shells) * (2 * slots) + wanted // shells
    pick = (jnp.asarray(place, jnp.int32)[:, None] == jnp.arange(wanted.size, dtype=jnp.int32)).astype(jnp.bfloat16)
    vmem = pl.BlockSpec(memory_space=pltpu.VMEM)
    return pl.pallas_call(
        functools.partial(solve_kernel, first=first, slots=slots, size=size),
        grid=(slots,),
        in_specs=[
            pl.BlockSpec(memory_space=pltpu.SMEM),
            vmem,
            vmem,
            pl.BlockSpec((1, lat, degrees), lambda s: (first + s, 0, 0)),
            vmem,
            vmem,
            vmem,
        ],
        out_specs=vmem,
        out_shape=jax.ShapeDtypeStruct(state.shape, jnp.float32),
        scratch_shapes=[
            pltpu.VMEM((slots, 4 * shells, lat), jnp.bfloat16),
            pltpu.VMEM((degrees, LANES), jnp.float32),
        ],
        compiler_params=pltpu.CompilerParams(vmem_limit_bytes=60 * 1024 * 1024),
        name="legendre_solve",
    )(bounds, modes, pick, legendre, coef, lanes, state)


def body(nonlinear_samples, legendre, assign, counts, spectral_state, inverses):
    rad_local, fields, lat_local, lon_count = nonlinear_samples.shape
    order_total = assign.shape[0]
    order_local = legendre.shape[0]
    degree_local = spectral_state.shape[0]
    shells = spectral_state.shape[2] // 4
    size = inverses.shape[2]
    bands = lax.axis_size("lat")
    devices = lax.axis_size("rad")
    lat_total = lat_local * bands

    rows = nonlinear_samples.reshape(rad_local * fields * lat_local, lon_count)
    orders = jnp.repeat(assign, 2)
    quarter = jnp.arange(2 * order_total, dtype=jnp.int32) % 2
    modes = fourier(trig_factors(orders, quarter, lon_count), rows)
    modes = modes.reshape(devices, 2 * order_local, rows.shape[0])
    moved = lax.all_to_all(modes, "rad", split_axis=0, concat_axis=0, tiled=True)
    if bands > 1:
        legendre = lax.all_to_all(legendre, "lat", split_axis=2, concat_axis=1, tiled=True)
        moved = moved.reshape(devices, 2 * order_local, fields, lat_local)
        moved = lax.all_gather(moved, "lat", axis=3, tiled=True)
    moved = moved.reshape(devices * 2 * order_local, fields * lat_total)

    rad_position = lax.axis_index("rad")
    lat_position = lax.axis_index("lat")
    mine = lax.dynamic_slice_in_dim(assign, rad_position * order_local, order_local, 0)
    ids = jnp.arange(order_total, dtype=jnp.int32)
    live = jnp.sum(jnp.where(mine[:, None] == ids[None, :], counts[None, :], 0), axis=1)
    offset = jnp.broadcast_to(lat_position * degree_local, mine.shape).astype(jnp.int32)
    bounds = jnp.stack([mine, mine + live, offset])

    coef = spread(coefficient_rows(inverses, shells))
    state = spectral_state.reshape(degree_local * order_local, 4 * shells)
    out = legendre_solve(bounds, moved, legendre, coef, lane_constants(shells), state, 0, order_local, size)
    return out.reshape(spectral_state.shape)


def solution(mesh):
    return jax.shard_map(
        body,
        mesh=mesh,
        in_specs=(
            P("rad", None, "lat", None),
            P("rad", "lat", None),
            P(),
            P(),
            P("lat", "rad", None),
            P("lat", None, None, None),
        ),
        out_specs=P("lat", "rad", None),
        check_vma=False,
    )
```

```python
import functools
import math

import jax
import jax.numpy as jnp
import numpy as np
from jax import lax
from jax.experimental import pallas as pl
from jax.experimental.pallas import tpu as pltpu
from jax.sharding import PartitionSpec as P

LANES = 128


def trig_factors(orders, quarter, lon_count):
    step = 2.0 * math.pi / lon_count
    coarse_count = lon_count // LANES
    coarse = (orders[:, None] * jnp.arange(coarse_count, dtype=jnp.int32)) % coarse_count * LANES
    fine = orders[:, None] * jnp.arange(LANES, dtype=jnp.int32) + quarter[:, None] * (lon_count // 4)
    coarse_angle = coarse.astype(jnp.float32) * step
    fine_angle = (fine % lon_count).astype(jnp.float32) * step
    scale = 1.0 / math.sqrt(lon_count)
    return (
        jnp.cos(coarse_angle),
        jnp.sin(coarse_angle),
        jnp.cos(fine_angle) * scale,
        jnp.sin(fine_angle) * scale,
    )


def fourier_kernel(ca, sa, cb, sb, x, out, table):
    @pl.when(pl.program_id(0) == 0)
    def _():
        for a in range(ca.shape[1]):
            value = ca[:, a : a + 1] * cb[...] - sa[:, a : a + 1] * sb[...]
            table[:, a * LANES : (a + 1) * LANES] = value.astype(jnp.bfloat16)

    out[...] = lax.dot_general(
        table[...], x[...], (((1,), (1,)), ((), ())), preferred_element_type=jnp.float32
    ).astype(jnp.bfloat16)


def fourier(factors, rows):
    modes = factors[0].shape[0]
    count, lon_count = rows.shape
    tile = 512 if count % 512 == 0 else count
    whole = lambda v: pl.BlockSpec(v.shape, lambda i: (0, 0))
    return pl.pallas_call(
        fourier_kernel,
        grid=(count // tile,),
        in_specs=[whole(v) for v in factors] + [pl.BlockSpec((tile, lon_count), lambda i: (i, 0))],
        out_specs=pl.BlockSpec((modes, tile), lambda i: (0, i)),
        out_shape=jax.ShapeDtypeStruct((modes, count), jnp.bfloat16),
        scratch_shapes=[pltpu.VMEM((modes, lon_count), jnp.bfloat16)],
        name="fourier",
    )(*factors, rows)


def lane_constants(shells):
    spacing = 0.65 / (shells + 1)
    shell = np.arange(LANES) % shells
    radius = 0.35 + 0.65 * (shell + 1.0) / (shells + 1)
    half = 0.5 * spacing / radius
    table = np.zeros((8, LANES), np.float32)
    table[0] = np.where(shell < shells - 1, 0.5 + half, 0.0)
    table[1] = np.where(shell > 0, 0.5 - half, 0.0)
    table[2] = -0.5 * spacing * spacing / (radius * radius)
    return jnp.asarray(table)


def explicit_kernel(offset, lanes, state, out, *, slots):
    tile = out.shape[2]
    start = offset[0] + pl.program_id(0) * tile
    degree = lax.broadcasted_iota(jnp.int32, (tile, LANES), 0) + start
    term = (degree * (degree + 1)).astype(jnp.float32) * lanes[2:3, :]
    for s in range(slots):
        now = state[pl.ds(s, tile, stride=slots), :]
        right = lanes[0:1, :] * pltpu.roll(now, LANES - 1, 1) + lanes[1:2, :] * pltpu.roll(now, 1, 1)
        out[s] = jnp.transpose(right + term * now)


def explicit_part(offset, lanes, state, slots):
    degrees = state.shape[0] // slots
    tile = min(LANES, degrees)
    return pl.pallas_call(
        functools.partial(explicit_kernel, slots=slots),
        grid=(degrees // tile,),
        in_specs=[
            pl.BlockSpec(memory_space=pltpu.SMEM),
            pl.BlockSpec(lanes.shape, lambda i: (0, 0)),
            pl.BlockSpec((tile * slots, LANES), lambda i: (i, 0)),
        ],
        out_specs=pl.BlockSpec((slots, LANES, tile), lambda i: (0, 0, i)),
        out_shape=jax.ShapeDtypeStruct((slots, LANES, degrees), jnp.float32),
        name="explicit_part",
    )(offset, lanes, state)


def solve_kernel(bounds, modes, pick, legendre, inv, explicit, *rest, first, slots, size, links, aliased):
    if aliased:
        rest = rest[1:]
    out, arranged, right = rest
    slot = pl.program_id(0)
    lat, degrees = legendre.shape[1:]
    half = arranged.shape[1] // 2
    blocks = len(links[0])
    comps = LANES // (blocks * size)

    @pl.when(slot == 0)
    def _():
        for f in range(2):
            part = jnp.dot(
                pick[...], modes[:, f * lat : (f + 1) * lat], preferred_element_type=jnp.float32
            ).astype(jnp.bfloat16)
            for s in range(slots):
                arranged[s, f * half : (f + 1) * half, :] = part[s * half : (s + 1) * half]

    mine = first + slot
    low = bounds[0, mine]
    high = bounds[1, mine]
    offset = bounds[2, 0]
    product = jnp.dot(arranged[slot], legendre[0], preferred_element_type=jnp.float32)
    degree = lax.broadcasted_iota(jnp.int32, product.shape, 1) + offset
    live = (degree >= low) & (degree < high)
    source = product.astype(jnp.bfloat16).astype(jnp.float32)
    right[...] = explicit[0] + jnp.where(live, source, 0.0)

    tile = min(LANES, degrees)
    total = out.shape[0] // degrees

    def piece(n, carry):
        start = pl.multiple_of(n * tile, tile)
        here = pl.ds(start, tile)
        solved = [[None] * blocks for _ in range(comps)]
        for k in range(blocks):
            matrix = [inv[(k * size + j) * size : (k * size + j + 1) * size, here] for j in range(size)]
            for c in range(comps):
                base = (c * blocks + k) * size
                lead = right[base : base + 1, here]
                if k:
                    lead = lead - links[0][k] * solved[c][k - 1][size - 1 : size]
                value = matrix[0] * lead
                for j in range(1, size):
                    value = value + matrix[j] * right[base + j : base + j + 1, here]
                solved[c][k] = value
        for k in range(blocks - 2, -1, -1):
            last = inv[(k + 1) * size * size - size : (k + 1) * size * size, here]
            for c in range(comps):
                solved[c][k] = solved[c][k] - links[1][k] * solved[c][k + 1][0:1] * last
        whole = jnp.concatenate([solved[c][k] for c in range(comps) for k in range(blocks)], axis=0)
        out[pl.ds(start * total + mine, tile, stride=total), :] = jnp.transpose(whole)
        return carry

    lax.fori_loop(0, degrees // tile, piece, 0)


def legendre_solve(bounds, modes, legendre, inv, explicit, previous, first, slots, size):
    shells = modes.shape[0] // (2 * slots)
    order, lat, degrees = legendre.shape
    spacing = 0.65 / (shells + 1)
    radius = 0.35 + 0.65 * (np.arange(shells) + 1.0) / (shells + 1)
    ratios = spacing / radius
    lower = [float(v) for v in -0.5 * (1.0 - ratios[0::size])]
    upper = [float(v) for v in -0.5 * (1.0 + ratios[size - 1 :: size])]
    wanted = np.arange(2 * slots * shells)
    place = (wanted % shells) * (2 * slots) + wanted // shells
    pick = (jnp.asarray(place, jnp.int32)[:, None] == jnp.arange(wanted.size, dtype=jnp.int32)).astype(jnp.bfloat16)
    vmem = pl.BlockSpec(memory_space=pltpu.VMEM)
    in_specs = [
        pl.BlockSpec(memory_space=pltpu.SMEM),
        vmem,
        vmem,
        pl.BlockSpec((1, lat, degrees), lambda s: (first + s, 0, 0)),
        vmem,
        pl.BlockSpec((1, LANES, degrees), lambda s: (first + s, 0, 0)),
    ]
    args = [bounds, modes, pick, legendre, inv, explicit]
    if previous is not None:
        in_specs.append(vmem)
        args.append(previous)
    return pl.pallas_call(
        functools.partial(
            solve_kernel, first=first, slots=slots, size=size, links=(lower, upper), aliased=previous is not None
        ),
        grid=(slots,),
        in_specs=in_specs,
        out_specs=vmem,
        out_shape=jax.ShapeDtypeStruct((degrees * order, LANES), jnp.float32),
        scratch_shapes=[
            pltpu.VMEM((slots, 4 * shells, lat), jnp.bfloat16),
            pltpu.VMEM((LANES, degrees), jnp.float32),
        ],
        input_output_aliases={6: 0} if previous is not None else {},
        compiler_params=pltpu.CompilerParams(vmem_limit_bytes=60 * 1024 * 1024),
        name="legendre_solve",
    )(*args)


def body(nonlinear_samples, legendre, assign, counts, spectral_state, inverses):
    rad_local, fields, lat_local, lon_count = nonlinear_samples.shape
    order_total = assign.shape[0]
    order_local = legendre.shape[0]
    degree_local = spectral_state.shape[0]
    shells = spectral_state.shape[2] // 4
    size = inverses.shape[2]
    bands = lax.axis_size("lat")
    devices = lax.axis_size("rad")
    lat_total = lat_local * bands

    rows = nonlinear_samples.reshape(rad_local * fields * lat_local, lon_count)
    orders = jnp.repeat(assign, 2)
    quarter = jnp.arange(2 * order_total, dtype=jnp.int32) % 2
    modes = fourier(trig_factors(orders, quarter, lon_count), rows)
    modes = modes.reshape(devices, 2 * order_local, rows.shape[0])
    moved = lax.all_to_all(modes, "rad", split_axis=0, concat_axis=0, tiled=True)
    if bands > 1:
        legendre = lax.all_to_all(legendre, "lat", split_axis=2, concat_axis=1, tiled=True)
        moved = moved.reshape(devices, 2 * order_local, fields, lat_local)
        moved = lax.all_gather(moved, "lat", axis=3, tiled=True)
    moved = moved.reshape(devices * 2 * order_local, fields * lat_total)

    rad_position = lax.axis_index("rad")
    lat_position = lax.axis_index("lat")
    mine = lax.dynamic_slice_in_dim(assign, rad_position * order_local, order_local, 0)
    ids = jnp.arange(order_total, dtype=jnp.int32)
    live = jnp.sum(jnp.where(mine[:, None] == ids[None, :], counts[None, :], 0), axis=1)
    offset = jnp.broadcast_to(lat_position * degree_local, mine.shape).astype(jnp.int32)
    bounds = jnp.stack([mine, mine + live, offset])

    inv = jnp.transpose(inverses, (1, 3, 2, 0)).reshape(-1, degree_local)
    state = spectral_state.reshape(degree_local * order_local, 4 * shells)
    explicit = explicit_part(offset[:1], lane_constants(shells), state, order_local)
    out = legendre_solve(bounds, moved, legendre, inv, explicit, None, 0, order_local, size)
    return out.reshape(spectral_state.shape)


def solution(mesh):
    return jax.shard_map(
        body,
        mesh=mesh,
        in_specs=(
            P("rad", None, "lat", None),
            P("rad", "lat", None),
            P(),
            P(),
            P("lat", "rad", None),
            P("lat", None, None, None),
        ),
        out_specs=P("lat", "rad", None),
        check_vma=False,
    )
```
